32 devices in a mesh: pipe: 2 (over core), gx: 4 (over y, x), gy: 4 (over z).
Axes of the slice: x: 2, y: 2, z: 4, core: 2. Of those that a mesh axis runs over, the one named last changes fastest.
Arguments:
- layer_input: bfloat16 [2, 512, 2304], P(None, 'gx', 'gy'), may hold values from -6 to 6
- cotangent: bfloat16 [2, 512, 2304], P(None, 'gx', 'gy'), may hold values from -6 to 6
- segments: int32 [2, 512], P(None, 'gx'), may hold values from 0 to 127, as said below
- query_weight: bfloat16 [2, 2304, 2048], P('pipe', 'gx', 'gy'), may hold values from -0.125 to 0.125
- key_weight: bfloat16 [2, 2304, 1024], P('pipe', 'gx', 'gy'), may hold values from -0.125 to 0.125
- value_weight: bfloat16 [2, 2304, 1024], P('pipe', 'gx', 'gy'), may hold values from -0.125 to 0.125
- out_weight: bfloat16 [2, 2048, 2304], P('pipe', 'gy', 'gx'), may hold values from -0.125 to 0.125
- gate_weight: bfloat16 [2, 2304, 9216], P('pipe', 'gx', 'gy'), may hold values from -0.125 to 0.125
- up_weight: bfloat16 [2, 2304, 9216], P('pipe', 'gx', 'gy'), may hold values from -0.125 to 0.125
- down_weight: bfloat16 [2, 9216, 2304], P('pipe', 'gy', 'gx'), may hold values from -0.0625 to 0.0625
- norm_gains: bfloat16 [2, 4, 2304], P('pipe', None, 'gy'), may hold values from 0.099609375 to 1.8984375
Outputs:
- section_out: bfloat16 [2, 2, 512, 2304], P('pipe', None, 'gx', 'gy')
- input_grad: bfloat16 [2, 2, 512, 2304], P('pipe', None, 'gx', 'gy')
- grad_query: float32 [2, 2304, 2048], P('pipe', 'gx', 'gy')
- grad_key: float32 [2, 2304, 1024], P('pipe', 'gx', 'gy')
- grad_value: float32 [2, 2304, 1024], P('pipe', 'gx', 'gy')
- grad_out: float32 [2, 2048, 2304], P('pipe', 'gy', 'gx')
- grad_gate: float32 [2, 2304, 9216], P('pipe', 'gx', 'gy')
- grad_up: float32 [2, 2304, 9216], P('pipe', 'gx', 'gy')
- grad_down: float32 [2, 9216, 2304], P('pipe', 'gy', 'gx')
- grad_gains: float32 [2, 4, 2304], P('pipe', None, 'gy')
The draws below stay inside these ranges and needn't reach their ends.
Inputs may be any that keep to these rules, and one draw needn't show every extreme that they name: `segments`: within each aligned block of 128 tokens of a micro-batch the ids start at 0 and rise by one where a new sequence begins; no sequence crosses a block, each has at most 128 tokens, and one has exactly 128. Every draw reaches the largest id.
All inputs are finite; a program needn't handle non-finite values.
Results may differ from the reference program's by a relative error of at most 0.035.
Values may be sent and summed in bfloat16 or wider, within the bound.
No kernel may reach another device: no remote copies, remote signals or barrier semaphores. Data moves between devices by JAX's collectives and lax.ppermute only.
A program may use at most 256 MiB of HBM per device.

```python
import jax
import jax.numpy as jnp
from jax import lax

D = 2304
HQ = 8
KV = 4
HD = 256
FF = 9216
TOK_DEV = 128
MB = 2
TOKENS = 512
SEQ_MOST = 128
N_PIPE = 2


def draw_segments(key, part):
    blocks = TOKENS // TOK_DEV
    rate_key = jax.random.fold_in(key, 11)
    start_key = jax.random.fold_in(key, 12)
    pick_key = jax.random.fold_in(key, 13)
    tiny_key = jax.random.fold_in(key, 14)
    level = jax.random.randint(rate_key, (MB, blocks, 1), 0, 5)
    chance = jax.random.randint(start_key, (MB, blocks, TOK_DEV), 0, 64)
    places = jnp.arange(TOK_DEV, dtype=jnp.int32)
    forced = places % SEQ_MOST == 0
    starts = (chance < jnp.left_shift(jnp.ones_like(level), level)) | forced[None, None, :]
    chosen = jax.random.randint(pick_key, (), 0, blocks)
    single = (jnp.arange(MB, dtype=jnp.int32)[:, None, None] == 0) & (jnp.arange(blocks, dtype=jnp.int32)[None, :, None] == chosen)
    starts = jnp.where(single, forced[None, None, :], starts)
    tiny_block = jax.random.randint(tiny_key, (), 0, blocks)
    every = (jnp.arange(MB, dtype=jnp.int32)[:, None, None] == MB - 1) & (jnp.arange(blocks, dtype=jnp.int32)[None, :, None] == tiny_block)
    starts = jnp.where(every, jnp.ones_like(starts), starts)
    seg_ids = jnp.cumsum(starts.astype(jnp.int32), axis=2) - 1
    return seg_ids.reshape(MB, TOKENS).astype(jnp.int32)


def block_levels(rng, shape, shards, low, top_value):
    loudness, own = 1.0, jax.random.fold_in(rng, 6)
    for dim, shards_of in shards:
        heights = jnp.exp(jax.random.uniform(jax.random.fold_in(own, dim), (shards_of,), jnp.float32, low / len(shards), top_value / len(shards)))
        loudness = loudness * jnp.repeat(heights, shape[dim] // shards_of).reshape([-1 if axis == dim else 1 for axis in range(len(shape))])
    return loudness


def normal_values(key, shape, deviation, bound, split=(), kind=jnp.bfloat16):
    drawn = jax.random.normal(key, shape, jnp.float32) * deviation
    if len(split) > 0:
        drawn = block_levels(key, shape, split, -0.22, 0.18) * drawn
    return jnp.clip(drawn, min=-bound, max=bound).astype(kind)


def setup_inputs(seed: int = 0) -> dict:
    streams_of = jax.random.split(jax.random.key(seed), 12)
    layer_input = normal_values(streams_of[0], (MB, TOKENS, D), 1.0, 6.0, ((1, 4), (2, 4)))
    cotangent = normal_values(streams_of[1], (MB, TOKENS, D), 1.0, 6.0, ((1, 4), (2, 4)))
    segments = draw_segments(jax.random.fold_in(streams_of[11], 71), 0)
    query_weight = normal_values(streams_of[3], (N_PIPE, D, HQ * HD), D ** -0.5, 0.125, ((0, 2), (1, 4), (2, 4)))
    key_weight = normal_values(streams_of[4], (N_PIPE, D, KV * HD), D ** -0.5, 0.125, ((0, 2), (1, 4), (2, 4)))
    value_weight = normal_values(streams_of[5], (N_PIPE, D, KV * HD), D ** -0.5, 0.125, ((0, 2), (1, 4), (2, 4)))
    out_weight = normal_values(streams_of[6], (N_PIPE, HQ * HD, D), (HQ * HD) ** -0.5, 0.125, ((0, 2), (1, 4), (2, 4)))
    gate_weight = normal_values(streams_of[7], (N_PIPE, D, FF), D ** -0.5, 0.125, ((0, 2), (1, 4), (2, 4)))
    up_weight = normal_values(streams_of[8], (N_PIPE, D, FF), D ** -0.5, 0.125, ((0, 2), (1, 4), (2, 4)))
    down_weight = normal_values(streams_of[9], (N_PIPE, FF, D), FF ** -0.5, 0.0625, ((0, 2), (1, 4), (2, 4)))
    norm_gains = jnp.clip(1.0 + 0.18 * jax.random.normal(streams_of[10], (N_PIPE, 4, D), jnp.float32), 0.099609375, 1.8984375).astype(jnp.bfloat16)
    return {"layer_input": layer_input, "cotangent": cotangent, "segments": segments, "query_weight": query_weight, "key_weight": key_weight, "value_weight": value_weight, "out_weight": out_weight, "gate_weight": gate_weight, "up_weight": up_weight, "down_weight": down_weight, "norm_gains": norm_gains}


epsilon = 1e-06
cap_value = 50.0
rope_base = 10000.0
query_scale = 0.0625

def to_half(value):
    return lax.optimization_barrier(value.astype(jnp.bfloat16))

def gelu_tanh(value):
    return 0.5 * value * (1.0 + jnp.tanh(0.7978845608028654 * (value + 0.044715 * value * value * value)))

def rope_tables(seg_ids):
    row_count = seg_ids.shape[0]
    places = jnp.arange(row_count, dtype=jnp.int32)
    same_doc = seg_ids[:, None] == seg_ids[None, :]
    earlier = jnp.where(same_doc & (places[None, :] < places[:, None]), 1.0, 0.0)
    position = lax.optimization_barrier(jnp.sum(earlier, axis=1))
    frequency = jnp.power(rope_base, -2.0 * jnp.arange(HD // 2, dtype=jnp.float32) / HD)
    angles = position[:, None] * frequency[None, :]
    allowed = same_doc & (places[None, :] <= places[:, None])
    return (jnp.cos(angles), jnp.sin(angles), allowed)

def rotate(value, cosine, sine_rows, direction):
    half_width = value.shape[-1] // 2
    first_half = value[..., :half_width]
    second_half = value[..., half_width:]
    cos_rows = cosine[:, None, :]
    sin_rows = sine_rows[:, None, :]
    return jnp.concatenate([first_half * cos_rows - direction * second_half * sin_rows, second_half * cos_rows + direction * first_half * sin_rows], axis=-1)

def outer_rows(left, right):
    return jnp.dot(left.T, right, preferred_element_type=jnp.float32)

def inner_cols(left, right):
    return jnp.dot(left, right.T, preferred_element_type=jnp.float32)

def inverse_rms(values):
    return lax.rsqrt(lax.optimization_barrier(jnp.mean(values * values, axis=1, keepdims=True)) + epsilon)

def norm_back(grad_rows, unit_rows, inverse, gain_row):
    scaled = grad_rows * gain_row
    mean_term = lax.optimization_barrier(jnp.mean(scaled * unit_rows, axis=1, keepdims=True))
    return (inverse * (scaled - unit_rows * mean_term), lax.optimization_barrier(jnp.sum(grad_rows * unit_rows, axis=0)))

def layer_forward(layer_in, weights, gain_rows, seg_ids):
    query_weight, key_weight, value_weight, out_weight, gate_weight, up_weight, down_weight = weights
    gain = gain_rows.astype(jnp.float32)
    cosine, sine_rows, allowed = rope_tables(seg_ids)
    row_count = layer_in.shape[0]
    group_size = HQ // KV
    whole_f = layer_in.astype(jnp.float32)
    norm_one = inverse_rms(whole_f)
    attn_input = to_half(whole_f * norm_one * gain[0])
    query_raw = jnp.dot(attn_input, query_weight, preferred_element_type=jnp.float32)
    key_raw = jnp.dot(attn_input, key_weight, preferred_element_type=jnp.float32)
    value_raw = jnp.dot(attn_input, value_weight, preferred_element_type=jnp.float32)
    query_rows = to_half((rotate(query_raw.reshape(row_count, HQ, HD), cosine, sine_rows, 1.0) * query_scale).reshape(row_count, KV, group_size, HD))
    key_rows = to_half(rotate(key_raw.reshape(row_count, KV, HD), cosine, sine_rows, 1.0))
    value_rows = to_half(value_raw.reshape(row_count, KV, HD))
    scores = jnp.einsum('tkgd,skd->kgts', query_rows.astype(jnp.float32), key_rows.astype(jnp.float32))
    capped = cap_value * jnp.tanh(scores / cap_value)
    log_total = jnp.log(lax.optimization_barrier(jnp.sum(jnp.where(allowed, jnp.exp(capped), 0.0), axis=-1)))
    attn_probs = to_half(jnp.where(allowed, jnp.exp(capped - log_total[..., None]), 0.0))
    context = to_half(jnp.einsum('kgts,skd->tkgd', attn_probs.astype(jnp.float32), value_rows.astype(jnp.float32)).reshape(row_count, HQ * HD))
    attn_sum = jnp.dot(context, out_weight, preferred_element_type=jnp.float32)
    norm_two = inverse_rms(attn_sum)
    residual = whole_f + attn_sum * norm_two * gain[1]
    norm_three = inverse_rms(residual)
    feed_input = to_half(residual * norm_three * gain[2])
    gate_sum = jnp.dot(feed_input, gate_weight, preferred_element_type=jnp.float32)
    up_sum = jnp.dot(feed_input, up_weight, preferred_element_type=jnp.float32)
    hidden = to_half(gelu_tanh(gate_sum) * up_sum)
    down_sum = jnp.dot(hidden, down_weight, preferred_element_type=jnp.float32)
    norm_four = inverse_rms(down_sum)
    layer_out = (residual + down_sum * norm_four * gain[3]).astype(jnp.bfloat16)
    kept = (whole_f, norm_one, attn_input, query_rows, key_rows, value_rows, log_total, context, attn_sum, norm_two, residual, norm_three, feed_input, gate_sum, up_sum, hidden, down_sum, norm_four)
    return (layer_out, kept)

def layer_backward(incoming, kept, weights, gain_rows, seg_ids):
    query_weight, key_weight, value_weight, out_weight, gate_weight, up_weight, down_weight = weights
    whole_f, norm_one, attn_input, query_rows, key_rows, value_rows, log_total, context, attn_sum, norm_two, residual, norm_three, feed_input, gate_sum, up_sum, hidden, down_sum, norm_four = kept
    gain = gain_rows.astype(jnp.float32)
    cosine, sine_rows, allowed = rope_tables(seg_ids)
    row_count = incoming.shape[0]
    resid_grad = incoming.astype(jnp.float32)
    down_grad, gain_four = norm_back(resid_grad, down_sum * norm_four, norm_four, gain[3])
    down_half = to_half(down_grad)
    hidden_grad = inner_cols(down_half, down_weight)
    term_down = outer_rows(hidden, down_half)
    activated, gelu_back = jax.vjp(gelu_tanh, gate_sum)
    gate_grad = to_half(gelu_back(hidden_grad * up_sum)[0])
    up_grad = to_half(hidden_grad * activated)
    term_gate = outer_rows(feed_input, gate_grad)
    term_up = outer_rows(feed_input, up_grad)
    feed_grad = inner_cols(gate_grad, gate_weight) + inner_cols(up_grad, up_weight)
    norm_grad, gain_three = norm_back(feed_grad, residual * norm_three, norm_three, gain[2])
    resid_grad = resid_grad + norm_grad
    attn_grad, gain_two = norm_back(resid_grad, attn_sum * norm_two, norm_two, gain[1])
    attn_half = to_half(attn_grad)
    context_grad = to_half(inner_cols(attn_half, out_weight)).reshape(row_count, KV, HQ // KV, HD)
    term_out = outer_rows(context, attn_half)
    query_f = query_rows.astype(jnp.float32)
    key_f = key_rows.astype(jnp.float32)
    scores = jnp.einsum('tkgd,skd->kgts', query_f, key_f)
    capped = cap_value * jnp.tanh(scores / cap_value)
    exact_probs = jnp.where(allowed, jnp.exp(capped - log_total[..., None]), 0.0)
    half_probs = to_half(exact_probs)
    context_f = context_grad.astype(jnp.float32)
    value_grad = jnp.einsum('kgts,tkgd->skd', half_probs.astype(jnp.float32), context_f)
    prob_grad = jnp.einsum('tkgd,skd->kgts', context_f, value_rows.astype(jnp.float32))
    row_dot = lax.optimization_barrier(jnp.sum(exact_probs * prob_grad, axis=-1, keepdims=True))
    ratio = capped / cap_value
    score_grad = to_half(exact_probs * (prob_grad - row_dot) * (1.0 - ratio * ratio)).astype(jnp.float32)
    query_grad = jnp.einsum('kgts,skd->tkgd', score_grad, key_f)
    key_grad = jnp.einsum('kgts,tkgd->skd', score_grad, query_f)
    query_half = to_half((rotate(query_grad.reshape(row_count, HQ, HD), cosine, sine_rows, -1.0) * query_scale).reshape(row_count, HQ * HD))
    key_half = to_half(rotate(key_grad, cosine, sine_rows, -1.0).reshape(row_count, KV * HD))
    value_half = to_half(value_grad.reshape(row_count, KV * HD))
    term_query = outer_rows(attn_input, query_half)
    term_key = outer_rows(attn_input, key_half)
    term_value = outer_rows(attn_input, value_half)
    first_grad = inner_cols(query_half, query_weight) + inner_cols(key_half, key_weight) + inner_cols(value_half, value_weight)
    first_norm, gain_one = norm_back(first_grad, whole_f * norm_one, norm_one, gain[0])
    input_back = (resid_grad + first_norm).astype(jnp.bfloat16)
    terms = (term_query, term_key, term_value, term_out, term_gate, term_up, term_down)
    return (input_back, terms, jnp.stack([gain_one, gain_two, gain_three, gain_four]))

def reference(layer_input, cotangent, segments, query_weight, key_weight, value_weight, out_weight, gate_weight, up_weight, down_weight, norm_gains):
    blocks = TOKENS // TOK_DEV
    stacked = (query_weight, key_weight, value_weight, out_weight, gate_weight, up_weight, down_weight)
    first_weights = tuple((weight[0] for weight in stacked))
    second_weights = tuple((weight[1] for weight in stacked))

    def by_block(array):
        shaped = array.reshape((MB, blocks, TOK_DEV) + array.shape[2:])
        return jnp.swapaxes(shaped, 0, 1)

    def one_block(carry, data):
        weight_totals, gain_totals = carry
        block_input, block_cot, block_seg = data
        first_terms = None
        second_terms = None
        gain_block = jnp.zeros((2, 4, D), jnp.float32)
        outs_block = []
        grads_block = []
        for batch_index in range(MB):
            seg_ids = block_seg[batch_index]
            first_out, first_kept = layer_forward(block_input[batch_index], first_weights, norm_gains[0], seg_ids)
            first_out = lax.optimization_barrier(first_out)
            second_out, second_kept = layer_forward(first_out, second_weights, norm_gains[1], seg_ids)
            second_back, second_new, second_gain = layer_backward(block_cot[batch_index], second_kept, second_weights, norm_gains[1], seg_ids)
            second_back = lax.optimization_barrier(second_back)
            first_back, first_new, first_gain = layer_backward(second_back, first_kept, first_weights, norm_gains[0], seg_ids)
            if first_terms is None:
                first_terms, second_terms = (first_new, second_new)
            else:
                first_terms = tuple((prior + fresh for prior, fresh in zip(first_terms, first_new)))
                second_terms = tuple((prior + fresh for prior, fresh in zip(second_terms, second_new)))
            gain_block = gain_block + jnp.stack([first_gain, second_gain])
            outs_block.append(jnp.stack([first_out, second_out]))
            grads_block.append(jnp.stack([first_back, second_back]))
        new_totals = tuple((total + jnp.stack([to_half(lower), to_half(upper)]).astype(jnp.float32) for total, lower, upper in zip(weight_totals, first_terms, second_terms)))
        return ((new_totals, gain_totals + gain_block), (jnp.stack(outs_block, axis=1), jnp.stack(grads_block, axis=1)))
    start_totals = tuple((jnp.zeros(weight.shape, jnp.float32) for weight in stacked))
    start_gains = jnp.zeros((2, 4, D), jnp.float32)
    (weight_totals, gain_totals), (outs_all, grads_all) = lax.scan(one_block, (start_totals, start_gains), (by_block(layer_input), by_block(cotangent), by_block(segments)))
    section_out = jnp.transpose(outs_all, (1, 2, 0, 3, 4)).reshape(2, MB, TOKENS, D)
    input_grad = jnp.transpose(grads_all, (1, 2, 0, 3, 4)).reshape(2, MB, TOKENS, D)
    return (section_out, input_grad, weight_totals[0], weight_totals[1], weight_totals[2], weight_totals[3], weight_totals[4], weight_totals[5], weight_totals[6], gain_totals)
```

```python
import jax
import jax.numpy as jnp
from jax import lax
from jax.sharding import PartitionSpec as P

D = 2304
HQ = 8
KV = 4
HD = 256
GROUP = HQ // KV

epsilon = 1e-06
cap_value = 50.0
rope_base = 10000.0
query_scale = 0.0625


f32 = jnp.float32
bf16 = jnp.bfloat16


def mm(a, b):
    return jnp.dot(a, b, preferred_element_type=f32)


def mm_t(a, b):
    return lax.dot_general(a, b, (((1,), (1,)), ((), ())), preferred_element_type=f32)


def outer(a, b):
    return lax.dot_general(a, b, (((0,), (0,)), ((), ())), preferred_element_type=f32)


def gelu_tanh(value):
    return (
        0.5
        * value
        * (1.0 + jnp.tanh(0.7978845608028654 * (value + 0.044715 * value * value * value)))
    )


def rotate(value, cosine, sine_rows, direction):
    half_width = value.shape[-1] // 2
    first_half = value[..., :half_width]
    second_half = value[..., half_width:]
    cos_rows = cosine[:, None, :]
    sin_rows = sine_rows[:, None, :]
    return jnp.concatenate(
        [
            first_half * cos_rows - direction * second_half * sin_rows,
            second_half * cos_rows + direction * first_half * sin_rows,
        ],
        axis=-1,
    )


class Grid:
    def __init__(self):
        self.n = lax.axis_size("gx")
        self.m = lax.axis_size("gy")
        self.i = lax.axis_index("gx")
        self.j = lax.axis_index("gy")
        self.c = lax.axis_index("pipe")

    def hop(self, value, axis, k):
        count = self.n if axis == "gx" else self.m
        return lax.ppermute(value, axis, [(s, s ^ k) for s in range(count)])

    def swap(self, value):
        return lax.ppermute(value, "pipe", [(0, 1), (1, 0)])

    def rs_gx(self, first, second):
        n = self.n
        first = first.reshape(n, -1, first.shape[-1])
        second = second.reshape(n, -1, second.shape[-1])
        if n != 4:
            out = []
            for part in (first, second):
                total = part[0].astype(f32)
                for k in range(1, n):
                    total = total + self.hop(part[k], "gx", k).astype(f32)
                out.append(total)
            return out
        from_x = self.hop(first[1::2], "gx", 1)
        from_y = self.hop(second[2:], "gx", 2)
        pass_y = (first[2].astype(f32) + from_x[1].astype(f32)).astype(bf16)
        pass_x = (second[1].astype(f32) + from_y[1].astype(f32)).astype(bf16)
        last_y = self.hop(pass_y, "gx", 2)
        last_x = self.hop(pass_x, "gx", 1)
        return [
            first[0].astype(f32) + from_x[0].astype(f32) + last_y.astype(f32),
            second[0].astype(f32) + from_y[0].astype(f32) + last_x.astype(f32),
        ]

    def ag_gx(self, value):
        n = self.n
        rows = value.shape[0]
        if n != 4:
            return jnp.concatenate([value] + [self.hop(value, "gx", k) for k in range(1, n)], 0)
        at_x = self.hop(value, "gx", 1)
        at_y = self.hop(value, "gx", 2)
        far_a = self.hop(at_x[: rows // 2], "gx", 2)
        far_b = self.hop(at_y[rows // 2 :], "gx", 1)
        return jnp.concatenate([value, at_x, at_y, far_a, far_b], 0)

    def psum_gx(self, value):
        n = self.n
        k = 1
        while k < n:
            other = self.hop(value, "gx", k)
            tiles = other.reshape(value.shape[0], n // (2 * k), 2, k, value.shape[1] // n)
            value = value + tiles[:, :, ::-1].reshape(value.shape)
            k *= 2
        return value

    def ar_gy(self, partial):
        n, m = self.n, self.m
        cols = partial.shape[-1]
        parts = partial.reshape(n, m, -1, cols)
        total = parts[:, 0].astype(f32)
        for k in range(1, m):
            total = total + self.hop(parts[:, k], "gy", k).astype(f32)
        mine = total.astype(bf16)
        return jnp.stack([mine] + [self.hop(mine, "gy", k) for k in range(1, m)], 1).reshape(
            -1, cols
        )


def row_sum(value):
    return jnp.sum(value, axis=1)


def layer_forward(grid, x, gain, weights, tables, extra=None):
    wq, wk, wv, wo, wg, wu, wd = weights
    cosine, sine_rows, allowed = tables
    block = allowed.shape[0]
    kv_local = wk.shape[1] // HD
    xf = x.astype(f32)
    a1 = (xf * gain[0]).astype(bf16)
    part_q = mm(a1, wq).astype(bf16)
    part_kv = mm(a1, jnp.concatenate([wk, wv], 1)).astype(bf16)
    rs1 = lax.rsqrt(grid.psum_gx(row_sum(xf * xf)[None])[0] / D + epsilon)
    sum_q, sum_kv = grid.rs_gx(part_q, part_kv)
    own1 = rs1[:block, None]
    sum_q = sum_q * own1
    sum_kv = sum_kv * own1
    query_rows = (
        (
            rotate(sum_q.reshape(block, kv_local * GROUP, HD), cosine, sine_rows, 1.0)
            * query_scale
        )
        .reshape(block, kv_local, GROUP, HD)
        .astype(bf16)
    )
    key_rows = rotate(
        sum_kv[:, : kv_local * HD].reshape(block, kv_local, HD), cosine, sine_rows, 1.0
    ).astype(bf16)
    value_rows = sum_kv[:, kv_local * HD :].reshape(block, kv_local, HD).astype(bf16)
    scores = jnp.einsum("tkgd,skd->kgts", query_rows, key_rows, preferred_element_type=f32)
    capped = cap_value * jnp.tanh(scores / cap_value)
    log_total = jnp.log(jnp.sum(jnp.where(allowed, jnp.exp(capped), 0.0), axis=-1))
    probs = jnp.where(allowed, jnp.exp(capped - log_total[..., None]), 0.0).astype(bf16)
    context = (
        jnp.einsum("kgts,skd->tkgd", probs, value_rows, preferred_element_type=f32)
        .astype(bf16)
        .reshape(block, kv_local * GROUP * HD)
    )
    context_all = grid.ag_gx(context)
    o = grid.ar_gy(mm(context_all, wo).astype(bf16)).astype(f32)
    rs2 = lax.rsqrt(grid.psum_gx(row_sum(o * o)[None])[0] / D + epsilon)
    r1 = xf + o * rs2[:, None] * gain[1]
    a3 = (r1 * gain[2]).astype(bf16)
    rs3 = lax.rsqrt(grid.psum_gx(row_sum(r1 * r1)[None])[0] / D + epsilon)
    own3 = rs3[:block, None]
    width = wg.shape[1]
    cut = width // 2
    gates, ups, hiddens, gathered = [], [], [], []
    for part in range(2):
        cols = slice(part * cut, (part + 1) * cut)
        gate, up = grid.rs_gx(mm(a3, wg[:, cols]).astype(bf16), mm(a3, wu[:, cols]).astype(bf16))
        gate = gate * own3
        up = up * own3
        hidden = (gelu_tanh(gate) * up).astype(bf16)
        gates.append(gate)
        ups.append(up)
        gathered.append(grid.ag_gx(hidden))
    down = mm(gathered[0], wd[:cut]) + mm(gathered[1], wd[cut:])
    f = grid.ar_gy(down.astype(bf16)).astype(f32)
    stats = [row_sum(f * f)]
    if extra is not None:
        stats.append(row_sum(extra * gain[3] * f))
    stats = grid.psum_gx(jnp.stack(stats))
    rs4 = lax.rsqrt(stats[0] / D + epsilon)
    m4 = stats[1] * rs4 / D if extra is not None else None
    out = (r1 + f * rs4[:, None] * gain[3]).astype(bf16)
    kept = dict(
        x=xf,
        rs1=rs1,
        a1=a1,
        q=query_rows,
        k=key_rows,
        v=value_rows,
        lse=log_total,
        ctx=context_all,
        o=o,
        rs2=rs2,
        r1=r1,
        rs3=rs3,
        a3=a3,
        gates=gates,
        ups=ups,
        hidden=gathered,
        f=f,
        rs4=rs4,
    )
    return out, kept, m4


def layer_backward(grid, c, m4, kept, gain, weights, tables, below=None):
    wq, wk, wv, wo, wg, wu, wd = weights
    cosine, sine_rows, allowed = tables
    block = allowed.shape[0]
    kv_local = wk.shape[1] // HD
    terms = {}
    w4 = kept["f"] * kept["rs4"][:, None]
    d_f = kept["rs4"][:, None] * (c * gain[3] - w4 * m4[:, None])
    dfh = d_f.astype(bf16)
    gain_four = jnp.sum(c * w4, axis=0)
    cut = wd.shape[0] // 2
    dh = grid.rs_gx(mm_t(dfh, wd[:cut]).astype(bf16), mm_t(dfh, wd[cut:]).astype(bf16))
    terms["down"] = (kept["hidden"], dfh)
    own3 = kept["rs3"][:block, None]
    d_gate, d_up = [], []
    for part in range(2):
        activated, gelu_back = jax.vjp(gelu_tanh, kept["gates"][part])
        scaled = dh[part] * own3
        d_gate.append(grid.ag_gx(gelu_back(scaled * kept["ups"][part])[0].astype(bf16)))
        d_up.append(grid.ag_gx((scaled * activated).astype(bf16)))
    da3 = (
        mm_t(d_gate[0], wg[:, :cut])
        + mm_t(d_up[0], wu[:, :cut])
        + mm_t(d_gate[1], wg[:, cut:])
        + mm_t(d_up[1], wu[:, cut:])
    )
    terms["gate"] = (kept["a3"], d_gate)
    terms["up"] = (kept["a3"], d_up)
    da3 = grid.ar_gy(da3.astype(bf16)).astype(f32)
    w3 = kept["r1"] * kept["rs3"][:, None]
    w2 = kept["o"] * kept["rs2"][:, None]
    gw2 = gain[1] * w2
    scaled3 = da3 * gain[2]
    stats = grid.psum_gx(
        jnp.stack([row_sum(scaled3 * w3), row_sum((c + scaled3) * gw2), row_sum(w3 * gw2)])
    )
    m3 = stats[0] / D
    m2 = (stats[1] - m3 * stats[2]) / D
    dr = c + scaled3 - w3 * m3[:, None]
    gain_three = jnp.sum(da3 * kept["r1"], axis=0)
    doh = (kept["rs2"][:, None] * (dr * gain[1] - w2 * m2[:, None])).astype(bf16)
    gain_two = jnp.sum(dr * w2, axis=0)
    half = wo.shape[0] // 2
    dctx = grid.rs_gx(mm_t(doh, wo[:half]).astype(bf16), mm_t(doh, wo[half:]).astype(bf16))
    terms["out"] = (kept["ctx"], doh)
    context_grad = (
        jnp.concatenate(dctx, 1).astype(bf16).reshape(block, kv_local, GROUP, HD)
    )
    query_rows, key_rows, value_rows = kept["q"], kept["k"], kept["v"]
    scores = jnp.einsum("tkgd,skd->kgts", query_rows, key_rows, preferred_element_type=f32)
    capped = cap_value * jnp.tanh(scores / cap_value)
    exact_probs = jnp.where(allowed, jnp.exp(capped - kept["lse"][..., None]), 0.0)
    half_probs = exact_probs.astype(bf16)
    value_grad = jnp.einsum(
        "kgts,tkgd->skd", half_probs, context_grad, preferred_element_type=f32
    )
    prob_grad = jnp.einsum(
        "tkgd,skd->kgts", context_grad, value_rows, preferred_element_type=f32
    )
    row_dot = jnp.sum(exact_probs * prob_grad, axis=-1, keepdims=True)
    ratio = capped / cap_value
    score_grad = (exact_probs * (prob_grad - row_dot) * (1.0 - ratio * ratio)).astype(bf16)
    query_grad = jnp.einsum("kgts,skd->tkgd", score_grad, key_rows, preferred_element_type=f32)
    key_grad = jnp.einsum("kgts,tkgd->skd", score_grad, query_rows, preferred_element_type=f32)
    own1 = kept["rs1"][:block, None]
    query_half = (
        rotate(query_grad.reshape(block, kv_local * GROUP, HD), cosine, sine_rows, -1.0)
        * query_scale
    ).reshape(block, kv_local * GROUP * HD) * own1
    key_half = (
        rotate(key_grad, cosine, sine_rows, -1.0).reshape(block, kv_local * HD) * own1
    )
    value_half = value_grad.reshape(block, kv_local * HD) * own1
    dqkv = grid.ag_gx(jnp.concatenate([query_half, key_half, value_half], 1).astype(bf16))
    da1 = grid.ar_gy(
        mm_t(dqkv, jnp.concatenate([wq, wk, wv], 1)).astype(bf16)
    ).astype(f32)
    terms["qkv"] = (kept["a1"], dqkv)
    w1 = kept["x"] * kept["rs1"][:, None]
    scaled1 = da1 * gain[0]
    stats = [row_sum(scaled1 * w1)]
    if below is not None:
        low_kept, low_gain = below
        gw4 = low_gain[3] * low_kept["f"] * low_kept["rs4"][:, None]
        stats += [row_sum((dr + scaled1) * gw4), row_sum(w1 * gw4)]
    stats = grid.psum_gx(jnp.stack(stats))
    m1 = stats[0] / D
    m4_low = (stats[1] - m1 * stats[2]) / D if below is not None else None
    gain_one = jnp.sum(da1 * kept["x"], axis=0)
    back = (dr + scaled1 - w1 * m1[:, None]).astype(bf16)
    return back, m4_low, terms, jnp.stack([gain_one, gain_two, gain_three, gain_four])


def local(
    layer_input,
    cotangent,
    segments,
    query_weight,
    key_weight,
    value_weight,
    out_weight,
    gate_weight,
    up_weight,
    down_weight,
    norm_gains,
):
    grid = Grid()
    n, m, i, j, c = grid.n, grid.m, grid.i, grid.j, grid.c
    square = n == m
    block = layer_input.shape[1]
    total = n * block
    chunk = block // m
    width = D // n
    first = c == 0

    def both(*shards):
        pair = lax.all_gather(jnp.concatenate([s[0] for s in shards], 1), "pipe", axis=0)
        return pair

    wq, wk, wv, wo, wg, wu, wd = [
        lax.all_gather(w[0], "pipe", axis=0)
        for w in (
            query_weight,
            key_weight,
            value_weight,
            out_weight,
            gate_weight,
            up_weight,
            down_weight,
        )
    ]
    gains = lax.all_gather(
        lax.all_gather(norm_gains[0], "gy", axis=1, tiled=True), "pipe", axis=0
    )
    gains = lax.dynamic_slice_in_dim(gains, i * width, width, 2).astype(f32)

    ar = jnp.arange(total, dtype=jnp.int32)
    kx = ar // block
    kz = (ar % block) // chunk
    r = ar % chunk
    source_block = i ^ kx
    source_row = (j ^ kz) * chunk + r
    if square:
        source = (source_block ^ j) * block + source_row
    else:
        source = source_block * block + source_row
    pick_in = (source[:, None] == ar[None, :]).astype(bf16)

    def spread(shard):
        if square:
            turned = lax.ppermute(
                shard, ("gx", "gy"), [(a * m + b, b * m + a) for a in range(n) for b in range(m)]
            )
            rows = jnp.concatenate(
                [turned] + [grid.hop(turned, "gy", k) for k in range(1, m)], 0
            )
        else:
            rows = lax.all_gather(shard, "gx", axis=0, tiled=True)
            rows = lax.all_gather(rows, "gy", axis=1, tiled=True)
            rows = lax.dynamic_slice_in_dim(rows, i * width, width, 1)
        return mm(pick_in, rows).astype(bf16)

    x_own = lax.dynamic_index_in_dim(layer_input, c, 0, keepdims=False)
    cot_own = lax.dynamic_index_in_dim(cotangent, c, 0, keepdims=False)
    seg_own = lax.dynamic_index_in_dim(segments, c, 0, keepdims=False)
    x0 = spread(x_own)
    cot = spread(cot_own)

    places = source_row[:block]
    pick = places[:, None] == jnp.arange(block, dtype=jnp.int32)[None, :]
    seg_rows = jnp.sum(jnp.where(pick, seg_own[None, :], 0), axis=1)
    same_doc = seg_rows[:, None] == seg_rows[None, :]
    earlier = jnp.where(same_doc & (places[None, :] < places[:, None]), 1.0, 0.0)
    position = jnp.sum(earlier, axis=1)
    frequency = jnp.power(rope_base, -2.0 * jnp.arange(HD // 2, dtype=f32) / HD)
    angles = position[:, None] * frequency[None, :]
    allowed = same_doc & (places[None, :] <= places[:, None])
    tables = (jnp.cos(angles), jnp.sin(angles), allowed)

    low = [w[0] for w in (wq, wk, wv, wo, wg, wu, wd)]
    high = [w[1] for w in (wq, wk, wv, wo, wg, wu, wd)]
    cot_f = cot.astype(f32)
    x1, kept0, _ = layer_forward(grid, x0, gains[0], low, tables)
    x2, kept1, m4 = layer_forward(grid, x1, gains[1], high, tables, cot_f)
    back1, m4_low, terms1, gain1 = layer_backward(
        grid, cot_f, m4, kept1, gains[1], high, tables, (kept0, gains[0])
    )
    back0, _, terms0, gain0 = layer_backward(
        grid, back1.astype(f32), m4_low, kept0, gains[0], low, tables
    )

    def place(of_low, of_high):
        own = jnp.where(first, of_low, of_high)
        other = jnp.where(first, of_high, of_low)
        if square:
            slot = i ^ j
            here = jnp.arange(block, dtype=jnp.int32)
            wanted = slot * block + (j ^ (here // chunk)) * chunk + here % chunk
            select = (wanted[:, None] == ar[None, :]).astype(bf16)
            axes = ("pipe", "gx", "gy")
            ranks = [(p, a, b) for p in range(2) for a in range(n) for b in range(m)]
            lin = lambda p, a, b: (p * n + a) * m + b
            own = lax.ppermute(
                mm(select, own).astype(bf16),
                axes,
                [(lin(p, a, b), lin(p, b, a)) for p, a, b in ranks],
            )
            other = lax.ppermute(
                mm(select, other).astype(bf16),
                axes,
                [(lin(p, a, b), lin(1 - p, b, a)) for p, a, b in ranks],
            )
        else:
            back_order = (source[None, :] == ar[:, None]).astype(bf16)
            span = D // m

            def shard(value):
                rows = mm(back_order, value).astype(bf16)
                rows = lax.all_gather(rows, "gx", axis=1, tiled=True)
                return lax.dynamic_slice(rows, (i * block, j * span), (block, span))

            own = shard(own)
            other = grid.swap(shard(other))
        return jnp.stack([jnp.where(first, own, other), jnp.where(first, other, own)])[None]

    section_out = place(x1, x2)
    input_grad = place(back0, back1)

    def grad(left_low, right_low, left_high, right_high):
        sent = outer(
            jnp.where(first, left_high, left_low), jnp.where(first, right_high, right_low)
        ).astype(bf16)
        held = outer(
            jnp.where(first, left_low, left_high), jnp.where(first, right_low, right_high)
        )
        return held + grid.swap(sent).astype(f32)

    def cat(parts):
        return jnp.concatenate(parts, 1)

    grad_down = jnp.concatenate(
        [
            grad(terms0["down"][0][p], terms0["down"][1], terms1["down"][0][p], terms1["down"][1])
            for p in range(2)
        ],
        0,
    )
    grad_gate = cat(
        [
            grad(terms0["gate"][0], terms0["gate"][1][p], terms1["gate"][0], terms1["gate"][1][p])
            for p in range(2)
        ]
    )
    grad_up = cat(
        [
            grad(terms0["up"][0], terms0["up"][1][p], terms1["up"][0], terms1["up"][1][p])
            for p in range(2)
        ]
    )
    grad_out = grad(*terms0["out"], *terms1["out"])
    grad_qkv = grad(*terms0["qkv"], *terms1["qkv"])
    q_cols = query_weight.shape[2]
    k_cols = key_weight.shape[2]
    grad_query = grad_qkv[:, :q_cols]
    grad_key = grad_qkv[:, q_cols : q_cols + k_cols]
    grad_value = grad_qkv[:, q_cols + k_cols :]

    gain_all = lax.all_gather(jnp.stack([gain0, gain1]), "gx", axis=2, tiled=True)
    gain_all = lax.dynamic_slice_in_dim(gain_all, j * (D // m), D // m, 2)
    gain_all = lax.psum(gain_all, "pipe")
    grad_gains = jnp.where(first, gain_all[0], gain_all[1])

    return (
        section_out,
        input_grad,
        grad_query[None],
        grad_key[None],
        grad_value[None],
        grad_out[None],
        grad_gate[None],
        grad_up[None],
        grad_down[None],
        grad_gains[None],
    )


def solution(mesh):
    in_specs = (
        P(None, "gx", "gy"),
        P(None, "gx", "gy"),
        P(None, "gx"),
        P("pipe", "gx", "gy"),
        P("pipe", "gx", "gy"),
        P("pipe", "gx", "gy"),
        P("pipe", "gy", "gx"),
        P("pipe", "gx", "gy"),
        P("pipe", "gx", "gy"),
        P("pipe", "gy", "gx"),
        P("pipe", None, "gy"),
    )
    out_specs = (
        P("pipe", None, "gx", "gy"),
        P("pipe", None, "gx", "gy"),
        P("pipe", "gx", "gy"),
        P("pipe", "gx", "gy"),
        P("pipe", "gx", "gy"),
        P("pipe", "gy", "gx"),
        P("pipe", "gx", "gy"),
        P("pipe", "gx", "gy"),
        P("pipe", "gy", "gx"),
        P("pipe", None, "gy"),
    )
    return jax.shard_map(local, mesh=mesh, in_specs=in_specs, out_specs=out_specs, check_vma=False)
```
